32 devices in a mesh: parts: 2 (over y), ctx: 4 (over z), mp: 4 (over x, core).
Axes of the slice: x: 2, y: 2, z: 4, core: 2. Of those that a mesh axis runs over, the one named last changes fastest.
Arguments:
- inputs: bfloat16 [1024, 3, 4096], P(('parts', 'ctx'), None, 'mp'), parts along dimension 0, may hold values from -6 to 6
- short_filter: bfloat16 [3, 3, 4096], P(None, None, 'mp'), may hold values from -3.5 to 3.5
- long_filter: bfloat16 [256, 128], P('mp'), may hold values from -0.5 to 0.5
- skip_gain: float32 [4096], P('mp'), may hold values from -1 to 1
- queries: bfloat16 [1024, 4096], P(('parts', 'ctx'), 'mp'), parts along dimension 0, may hold values from -6 to 6
- key_rows: bfloat16 [1024, 4096], P(('parts', 'ctx'), 'mp'), parts along dimension 0, may hold values from -6 to 6
- out_weight: bfloat16 [4096, 4096], P('mp'), may hold values from -0.25 to 0.25
Outputs:
- block_output: bfloat16 [1024, 4096], P(('parts', 'ctx'), 'mp'), parts along dimension 0
The draws below stay inside these ranges and needn't reach their ends.
There are 2 independent parts, one for each index of `parts`. The reference program is written for one: setup_inputs(seed, part) draws one part's arguments, and reference() takes and returns one part's arrays. A program takes and returns all parts, laid end to end along the dimension named above; an argument that names none is the same for every part. Nothing has to cross between parts.
All inputs are finite; a program needn't handle non-finite values.
Results may differ from the reference program's by a relative error of at most 0.014.
Values may be sent and summed in bfloat16 or wider, within the bound.
A program may use at most 64 MiB of HBM per device.

```python
import jax
import jax.numpy as jnp
from jax import lax

D = 4096
HEAD_DIM = 128
GROUP = 16
SHORT_K = 3
LONG_K = 128
GROUPS = 256
WINDOW = 512


def drawn_values(key, salt):
    return 1.5 * jax.random.truncated_normal(jax.random.fold_in(key, salt), -4.0, 4.0, (WINDOW, D), jnp.float32)


def draw_queries(key, part):
    values_drawn = drawn_values(key, 1)
    return values_drawn.astype(jnp.bfloat16)


def draw_key_rows(key, part):
    values_drawn = drawn_values(key, 2)
    return values_drawn.astype(jnp.bfloat16)


def raised(array, key, source, target, parts, factor):
    def block_of(position):
        return (jnp.arange(array.shape[position]) // (array.shape[position] // parts)).reshape((-1,) + (1,) * (array.ndim - 1 - position))

    first = jax.random.permutation(key, parts)[block_of(target)]
    other_side = (block_of(target) + parts // 2) % parts
    return jnp.where((block_of(source) == first) | (block_of(source) == other_side), factor * array, array)


def steps_of(rng, shape, cuts, smallest, largest):
    level, own = 1.0, jax.random.fold_in(rng, 6)
    for dim, shards_of in cuts:
        steps = jnp.exp(jax.random.uniform(jax.random.fold_in(own, dim), (shards_of,), jnp.float32, smallest / len(cuts), largest / len(cuts)))
        level = level * jnp.repeat(steps, shape[dim] // shards_of).reshape([-1 if axis == dim else 1 for axis in range(len(shape))])
    return level


def centred(own_key, dims, scale, reach, split=(), dtype=jnp.bfloat16):
    array = jax.random.normal(own_key, dims, jnp.float32) * scale
    if len(split) > 0:
        array = steps_of(own_key, dims, split, -0.22, 0.18) * array
    return jnp.clip(array, min=-reach, max=reach).astype(dtype)


def bell_draw_with(key, dims, width, limit, pieces, heavy, kind=jnp.bfloat16):
    values = width * jax.random.normal(key, dims, jnp.float32)
    if pieces:
        values = values * steps_of(key, dims, pieces, -0.22, 0.18)
    return jnp.clip(raised(values, jax.random.fold_in(key, 3), *heavy), -limit, limit).astype(kind)


def setup_inputs(seed: int = 0, part: int = 0) -> dict:
    splits = jax.random.split(jax.random.key(seed), 8)
    part_keys = jax.random.split(jax.random.fold_in(splits[7], part), 8)
    inputs = centred(part_keys[0], (WINDOW, 3, D), 1.0, 6.0, ((0, 4), (2, 4)))
    short_filter = centred(splits[1], (SHORT_K, 3, D), SHORT_K ** -0.5, 3.5, ((2, 4),))
    long_filter = centred(splits[2], (GROUPS, LONG_K), LONG_K ** -0.5, 0.5, ((0, 4),))
    skip_gain = jnp.clip(jax.random.uniform(splits[3], (D,), jnp.float32, -1.0, 1.0) * steps_of(splits[3], (D,), ((0, 4),), -0.4, 0.0), -1.0, 1.0)
    queries = draw_queries(jax.random.fold_in(jax.random.fold_in(splits[7], part), 71), part)
    key_rows = draw_key_rows(jax.random.fold_in(jax.random.fold_in(splits[7], part), 71), part)
    out_weight = bell_draw_with(splits[6], (D, D), (D // 4) ** -0.5, 0.25, ((0, 4),), (0, 1, 4, 2.0))
    return {"inputs": inputs, "short_filter": short_filter, "long_filter": long_filter, "skip_gain": skip_gain, "queries": queries, "key_rows": key_rows, "out_weight": out_weight}


def reference(inputs, short_filter, long_filter, skip_gain, queries, key_rows, out_weight):
    window = inputs.shape[0]
    signal = inputs.astype(jnp.float32)
    features = jnp.zeros(signal.shape, jnp.float32)
    for lag_index in range(SHORT_K):
        delayed = jnp.pad(signal, ((lag_index, 0), (0, 0), (0, 0)))[:window]
        features = features + short_filter[lag_index].astype(jnp.float32)[None] * delayed
    gate_product = (features[:, 1] * features[:, 2]).astype(jnp.bfloat16)
    gate_float = gate_product.astype(jnp.float32)
    filters = jnp.repeat(long_filter.astype(jnp.float32), GROUP, axis=0)
    padded = jnp.pad(gate_float, ((LONG_K - 1, 0), (0, 0)))

    def add_tap(tap_index, filtered):
        column = lax.dynamic_slice_in_dim(filters, tap_index, 1, 1)[:, 0]
        delayed = lax.dynamic_slice_in_dim(padded, LONG_K - 1 - tap_index, window, 0)
        return filtered + column[None] * delayed

    filtered = lax.fori_loop(0, LONG_K, add_tap, jnp.zeros((window, D), jnp.float32))
    values = (features[:, 0] * (filtered + skip_gain[None] * gate_float)).astype(jnp.bfloat16)
    head_count = D // HEAD_DIM
    head_queries = queries.reshape(window, head_count, HEAD_DIM).transpose(1, 0, 2)
    head_keys = key_rows.reshape(window, head_count, HEAD_DIM).transpose(1, 0, 2)
    head_values = values.reshape(window, head_count, HEAD_DIM).transpose(1, 0, 2)
    causal = jnp.tril(jnp.ones((window, window), jnp.bool_))

    def one_head(operands):
        head_query, head_key, head_value = operands
        scores = jnp.dot(head_query, head_key.T, preferred_element_type=jnp.float32) * (HEAD_DIM ** -0.5)
        new_max = jnp.max(jnp.where(causal, scores, -1e30), axis=1)
        probabilities = jnp.where(causal, jnp.exp(scores - new_max[:, None]), 0.0)
        weight_sum = jnp.sum(probabilities, axis=1)
        mixed = jnp.dot(probabilities.astype(jnp.bfloat16), head_value, preferred_element_type=jnp.float32)
        return (mixed / weight_sum[:, None]).astype(jnp.bfloat16)

    attended = lax.map(one_head, (head_queries, head_keys, head_values))
    attended = attended.transpose(1, 0, 2).reshape(window, D)
    return jnp.dot(attended, out_weight, preferred_element_type=jnp.float32).astype(jnp.bfloat16)
```

```python
import functools

import jax
import jax.numpy as jnp
from jax import lax
from jax.experimental import pallas as pl
from jax.experimental.pallas import tpu as pltpu
from jax.sharding import PartitionSpec as P

HD = 128
MESH = pl.DeviceIdType.MESH
NEG = -1e30
F32 = jnp.float32
BF = jnp.bfloat16


def dot(a, b, ca=1, cb=0):
    return lax.dot_general(a, b, (((ca,), (cb,)), ((), ())), preferred_element_type=F32)


def kernel(
    n, m, x_hbm, sf_ref, lf_ref, skip_ref, q_hbm, k_hbm, w_hbm, out_ref,
    xb, rim_out, rim_in, f0, gown, gprev, taps, kbuf, vbuf, qbuf, mst, lst, ast,
    sbuf, sstat, pbuf, pstat, att, wv, acc, s1, r1, s2, r2,
    xsem, qsem, ksem, wsem, rim_s, rim_r, gate_s, gate_r, k_s, k_r, v_s, v_r,
    q_s, q_r, o_s, o_r, t_s, t_r, a_s, a_r, b_s, b_r,
):
    z = lax.axis_index("ctx")
    me = lax.axis_index("mp")
    core = lax.rem(me, 2)
    chip = me // 2
    chips = m // 2
    partner = chip * 2 + 1 - core
    pivot = n // 3
    slots = n - pivot
    rows = xb.shape[1]
    heads = gown.shape[0]
    groups = lf_ref.shape[0]
    per_tile = groups // heads
    width = HD // per_tile
    tap_count = lf_ref.shape[1]
    short = sf_ref.shape[0]
    span = min(3, slots) * rows
    query_groups = qbuf.shape[1] // span
    cols = out_ref.shape[1]
    own = jnp.minimum(z, pivot)

    def remote(src, dst, ss, rs, axis, target):
        return pltpu.make_async_remote_copy(
            src_ref=src, dst_ref=dst, send_sem=ss, recv_sem=rs,
            device_id={axis: target}, device_id_type=MESH)

    local_x = pltpu.make_async_copy(x_hbm, xb, xsem)
    local_x.start()
    local_k, local_q = [], []
    for h in range(heads):
        part = pl.ds(h * HD, HD)
        local_k.append(pltpu.make_async_copy(k_hbm.at[:, part], kbuf.at[own, h], ksem.at[h]))
        local_q.append(pltpu.make_async_copy(q_hbm.at[:, part], qbuf.at[h, pl.ds(0, rows)], qsem.at[h]))
    for c in local_k + local_q:
        c.start()
    local_w = pltpu.make_async_copy(w_hbm, wv, wsem)
    local_w.start()

    barrier = pltpu.get_barrier_semaphore()
    count = jnp.int32(m - 1)
    for other in range(m):
        @pl.when(other != me)
        def _():
            pl.semaphore_signal(barrier, inc=1, device_id={"mp": other}, device_id_type=MESH)
    for other in range(n):
        low, high = jnp.minimum(z, other), jnp.maximum(z, other)
        talks = (low != high) & ((high == low + 1) | (high <= pivot) | (low >= pivot))
        count = count + talks.astype(jnp.int32)

        @pl.when(talks)
        def _():
            pl.semaphore_signal(barrier, inc=1, device_id={"ctx": other}, device_id_type=MESH)

    local_x.wait()
    for j in range(3):
        rim_out[2 * j:2 * j + 2, :] = xb[j, rows - 2:rows, :]

    @pl.when(z == 0)
    def _():
        rim_in[...] = jnp.zeros_like(rim_in)
        gprev[...] = jnp.zeros_like(gprev)

    pl.semaphore_wait(barrier, count)

    up = jnp.minimum(z + 1, n - 1)
    rim = remote(rim_out, rim_in, rim_s, rim_r, "ctx", up)
    gate = remote(gown, gprev, gate_s, gate_r, "ctx", up)

    @pl.when(z < n - 1)
    def _():
        rim.start()

    for c in local_k + local_q:
        c.wait()

    def each_query(act):
        for other in range(pivot, n - 1):
            @pl.when(other < z)
            def _():
                act(remote(
                    qbuf.at[:, pl.ds(0, rows)],
                    qbuf.at[:, pl.ds(pl.multiple_of((z - other) * rows, rows), rows)],
                    q_s.at[other - pivot], q_r.at[z - other], "ctx", other))

    def each_key(act):
        for other in range(1, pivot + 1):
            @pl.when((other > z) & (z < pivot))
            def _():
                act(remote(kbuf.at[own], kbuf.at[own], k_s.at[other], k_r.at[own], "ctx", other))

    def each_value(h, act):
        for other in range(1, pivot + 1):
            @pl.when((other > z) & (z < pivot))
            def _():
                act(remote(vbuf.at[own, h], vbuf.at[own, h], v_s.at[other, h], v_r.at[own, h], "ctx", other))

    each_query(lambda c: c.start())
    each_key(lambda c: c.start())

    @pl.when(z > 0)
    def _():
        rim.wait_recv()

    row = lax.broadcasted_iota(jnp.int32, (rows, HD), 0)

    @pl.loop(0, heads)
    def _(h):
        part = pl.ds(pl.multiple_of(h * HD, HD), HD)
        edge = rim_in[:, part].astype(F32)
        feats = []
        for j in range(3):
            x = xb[j, :, part].astype(F32)
            last = edge[2 * j + 1:2 * j + 2]
            x1 = jnp.where(row == 0, last, pltpu.roll(x, 1, 0))
            x2 = jnp.where(row == 0, edge[2 * j:2 * j + 1],
                           jnp.where(row == 1, last, pltpu.roll(x, 2, 0)))
            total = sf_ref[0, j:j + 1, part].astype(F32) * x
            total = total + sf_ref[1, j:j + 1, part].astype(F32) * x1
            feats.append(total + sf_ref[2, j:j + 1, part].astype(F32) * x2)
        f0[h] = feats[0]
        gown[h] = (feats[1] * feats[2]).astype(BF)

    @pl.when(z < n - 1)
    def _():
        gate.start()

    flip = (lax.broadcasted_iota(jnp.int32, (tap_count, 2 * rows), 0)
            + lax.broadcasted_iota(jnp.int32, (tap_count, 2 * rows), 1)) == rows
    based = dot(lf_ref[...], flip.astype(BF))
    for g in range(groups):
        wide = jnp.broadcast_to(based[g:g + 1], (rows, 2 * rows))
        taps[g] = pltpu.roll(wide, 0, 1, stride=1, stride_axis=0).astype(BF)
    acc[...] = jnp.zeros_like(acc)

    @pl.when(z > 0)
    def _():
        gate.wait_recv()

    lane = lax.broadcasted_iota(jnp.int32, (rows, HD), 1) // width

    @pl.loop(0, heads)
    def _(h):
        mine = gown[h]
        both = jnp.concatenate([gprev[h], mine], axis=0)
        filt = jnp.zeros((rows, HD), F32)
        for g in range(per_tile):
            filt = jnp.where(lane == g, dot(taps[h * per_tile + g], both), filt)
        part = pl.ds(pl.multiple_of(h * HD, HD), HD)
        val = f0[h] * (filt + skip_ref[:, part] * mine.astype(F32))
        vbuf[own, h] = val.T.astype(BF)
        each_value(h, lambda c: c.start())

    scale = HD ** -0.5
    krow = lax.broadcasted_iota(jnp.int32, (rows, span), 0)
    kcol = lax.broadcasted_iota(jnp.int32, (rows, span), 1)

    def each_part(h, act):
        for s in range(1, slots):
            @pl.when((z >= pivot) & (z + s < n))
            def _():
                act(s,
                    remote(sbuf.at[s - 1, h], pbuf.at[z - pivot, h],
                           o_s.at[s - 1, h], o_r.at[z - pivot, h], "ctx", z + s),
                    remote(sstat.at[s - 1, h], pstat.at[z - pivot, h],
                           t_s.at[s - 1, h], t_r.at[z - pivot, h], "ctx", z + s))

    def hand_over(h):
        def act(s, o, t):
            gi, at = (s * rows) // span, (s * rows) % span
            mm = mst[h, gi, :, at:at + rows]
            ll = lst[h, gi, :, at:at + rows]
            aa = ast[h, gi, :, at:at + rows]
            sbuf[s - 1, h] = (aa * (1.0 / ll[0:1])).astype(BF)
            sstat[s - 1, h] = mm + jnp.log(ll)
            o.start()
            t.start()
        each_part(h, act)

    for s in range(1, slots):
        @pl.when((z >= pivot) & (z + s < n))
        def _():
            pltpu.make_async_remote_copy(
                src_ref=qbuf.at[:, pl.ds(0, rows)], dst_ref=qbuf.at[:, pl.ds(s * rows, rows)],
                send_sem=q_s.at[0], recv_sem=q_r.at[s],
                device_id={"ctx": jnp.minimum(z + s, n - 1)}, device_id_type=MESH).wait_recv()

    @pl.loop(0, heads)
    def _(h):
        for gi in range(query_groups):
            q = qbuf[h, gi * span:(gi + 1) * span]
            s = dot(kbuf[own, h], q, 1, 1) * scale
            s = jnp.where(krow <= kcol + gi * span, s, NEG)
            mx = jnp.max(s, axis=0, keepdims=True)
            p = jnp.exp(s - mx)
            mst[h, gi] = jnp.broadcast_to(mx, (8, span))
            lst[h, gi] = jnp.broadcast_to(jnp.sum(p, axis=0, keepdims=True), (8, span))
            ast[h, gi] = dot(vbuf[own, h], p.astype(BF))

        @pl.when(z > pivot)
        def _():
            hand_over(h)

    @pl.when((z > 0) & (z <= pivot))
    def _():
        @pl.loop(0, z)
        def _(j):
            remote(kbuf.at[j], kbuf.at[j], k_s.at[0], k_r.at[j], "ctx", j).wait_recv()

    def one_head(h):
        @pl.loop(0, jnp.where(z <= pivot, z, 0))
        def _(j):
            remote(vbuf.at[j, h], vbuf.at[j, h], v_s.at[0, 0], v_r.at[j, h], "ctx", j).wait_recv()
            for gi in range(query_groups):
                q = qbuf[h, gi * span:(gi + 1) * span]
                s = dot(kbuf[j, h], q, 1, 1) * scale
                old = mst[h, gi, 0:1]
                mx = jnp.maximum(old, jnp.max(s, axis=0, keepdims=True))
                p = jnp.exp(s - mx)
                fade = jnp.exp(old - mx)
                mst[h, gi] = jnp.broadcast_to(mx, (8, span))
                lst[h, gi] = jnp.broadcast_to(
                    lst[h, gi, 0:1] * fade + jnp.sum(p, axis=0, keepdims=True), (8, span))
                ast[h, gi] = ast[h, gi] * fade + dot(vbuf[j, h], p.astype(BF))

        @pl.when(z == pivot)
        def _():
            hand_over(h)

        @pl.loop(0, jnp.maximum(z - pivot, 0))
        def _(j):
            remote(sbuf.at[0, 0], pbuf.at[j, h], o_s.at[0, 0], o_r.at[j, h], "ctx", j + pivot).wait_recv()
            remote(sstat.at[0, 0], pstat.at[j, h], t_s.at[0, 0], t_r.at[j, h], "ctx", j + pivot).wait_recv()
            old = mst[h, 0, :, 0:rows]
            lse = pstat[j, h]
            mx = jnp.maximum(old, lse)
            fade, gain = jnp.exp(old - mx), jnp.exp(lse - mx)
            mst[h, 0, :, 0:rows] = mx
            lst[h, 0, :, 0:rows] = lst[h, 0, :, 0:rows] * fade + gain
            ast[h, 0, :, 0:rows] = ast[h, 0, :, 0:rows] * fade[0:1] + pbuf[j, h].astype(F32) * gain[0:1]

        done = ast[h, 0, :, 0:rows] * (1.0 / lst[h, 0, 0:1, 0:rows])
        return done.T.astype(BF)

    @pl.loop(0, heads // 2)
    def _(c):
        att[c, :, 0:HD] = one_head(2 * c)
        att[c, :, HD:2 * HD] = one_head(2 * c + 1)

        @pl.when(c == 0)
        def _():
            local_w.wait()

        lhs = att[c]

        @pl.loop(0, m)
        def _(b):
            at = pl.ds(pl.multiple_of(b * cols, cols), cols)
            acc[b] += dot(lhs, wv[pl.ds(pl.multiple_of(c * 2 * HD, 2 * HD), 2 * HD), at])

    pieces = 4
    piece = cols // pieces

    def across(d, i):
        return remote(s1.at[d, i], r1.at[d, i], a_s.at[d, i], a_r.at[d, i], "mp", partner)

    def along(d, i):
        there = lax.rem(chip + d, chips) * 2 + core
        return remote(s2.at[d, i], r2.at[d, i], b_s.at[d, i], b_r.at[d, i], "mp", there)

    order = [d % chips for d in range(1, chips + 1)]
    for d in order:
        b = lax.rem(chip + d, chips) * 2 + 1 - core
        for i in range(pieces):
            s1[d, i] = acc[b, :, i * piece:(i + 1) * piece].astype(BF)
            across(d, i).start()
    for d in range(1, chips):
        b = lax.rem(chip + d, chips) * 2 + core
        for i in range(pieces):
            across(d, i).wait_recv()
            s2[d, i] = (acc[b, :, i * piece:(i + 1) * piece] + r1[d, i].astype(F32)).astype(BF)
            along(d, i).start()
    for i in range(pieces):
        across(0, i).wait_recv()
        total = acc[me, :, i * piece:(i + 1) * piece] + r1[0, i].astype(F32)
        for d in range(1, chips):
            along(d, i).wait_recv()
            total = total + r2[d, i].astype(F32)
        out_ref[:, i * piece:(i + 1) * piece] = total.astype(BF)

    for i in range(pieces):
        for d in range(chips):
            across(d, i).wait_send()
        for d in range(1, chips):
            along(d, i).wait_send()

    @pl.when(z < n - 1)
    def _():
        rim.wait_send()
        gate.wait_send()

    each_query(lambda c: c.wait_send())
    each_key(lambda c: c.wait_send())

    @pl.loop(0, heads)
    def _(h):
        def ended(s, o, t):
            o.wait_send()
            t.wait_send()
        each_value(h, lambda c: c.wait_send())
        each_part(h, ended)


def per_device(n, m, inputs, short_filter, long_filter, skip_gain, queries, key_rows, out_weight):
    rows, _, channels = inputs.shape
    heads = channels // HD
    groups = long_filter.shape[0]
    total = out_weight.shape[1]
    cols = total // m
    chips = m // 2
    pivot = n // 3
    slots = n - pivot
    batch = min(3, slots)
    padded = -(-slots // batch) * batch
    span = batch * rows
    gq = padded // batch
    parts = max(slots - 1, 1)
    vm = pltpu.VMEM
    dma = pltpu.SemaphoreType.DMA
    scratch = [
        vm((3, rows, channels), BF), vm((16, channels), BF), vm((16, channels), BF),
        vm((heads, rows, HD), F32), vm((heads, rows, HD), BF), vm((heads, rows, HD), BF),
        vm((groups, rows, 2 * rows), BF),
        vm((pivot + 1, heads, rows, HD), BF), vm((pivot + 1, heads, HD, rows), BF),
        vm((heads, padded * rows, HD), BF),
        vm((heads, gq, 8, span), F32), vm((heads, gq, 8, span), F32), vm((heads, gq, HD, span), F32),
        vm((parts, heads, HD, rows), BF), vm((parts, heads, 8, rows), F32),
        vm((parts, heads, HD, rows), BF), vm((parts, heads, 8, rows), F32),
        vm((heads // 2, rows, 2 * HD), BF), vm((channels, total), BF), vm((m, rows, cols), F32),
    ] + [vm((chips, 4, rows, cols // 4), BF)] * 4 + [
        dma, dma((heads,)), dma((heads,)), dma, dma, dma, dma, dma,
        dma((pivot + 1,)), dma((pivot + 1,)), dma((pivot + 1, heads)), dma((pivot + 1, heads)),
        dma((slots,)), dma((slots,)),
        dma((parts, heads)), dma((parts, heads)), dma((parts, heads)), dma((parts, heads)),
    ] + [dma((chips, 4))] * 4
    in_vmem = pl.BlockSpec(memory_space=pltpu.VMEM)
    in_hbm = pl.BlockSpec(memory_space=pl.ANY)
    return pl.pallas_call(
        functools.partial(kernel, n, m),
        out_shape=jax.ShapeDtypeStruct((rows, cols), BF),
        in_specs=[in_hbm, in_vmem, in_vmem, in_vmem, in_hbm, in_hbm, in_hbm],
        out_specs=in_vmem,
        scratch_shapes=scratch,
        compiler_params=pltpu.CompilerParams(
            collective_id=0, has_side_effects=True, vmem_limit_bytes=60 * 2**20),
    )(inputs.transpose(1, 0, 2), short_filter, long_filter, skip_gain[None], queries, key_rows, out_weight)


def solution(mesh):
    placed = (
        P(("parts", "ctx"), None, "mp"),
        P(None, None, "mp"),
        P("mp", None),
        P("mp"),
        P(("parts", "ctx"), "mp"),
        P(("parts", "ctx"), "mp"),
        P("mp", None),
    )
    return jax.shard_map(
        functools.partial(per_device, mesh.shape["ctx"], mesh.shape["mp"]),
        mesh=mesh, in_specs=placed, out_specs=P(("parts", "ctx"), "mp"), check_vma=False)
```

```python
import functools

import jax
import jax.numpy as jnp
from jax import lax
from jax.experimental import pallas as pl
from jax.experimental.pallas import tpu as pltpu
from jax.sharding import PartitionSpec as P

HD = 128
MESH = pl.DeviceIdType.MESH
NEG = -1e30
F32 = jnp.float32
BF = jnp.bfloat16


def dot(a, b, ca=1, cb=0):
    return lax.dot_general(a, b, (((ca,), (cb,)), ((), ())), preferred_element_type=F32)


def kernel(
    n, m, x_hbm, sf_ref, lf_ref, skip_ref, q_hbm, k_hbm, w_hbm, out_ref,
    xb, rim_out, rim_in, f0, gown, gprev, taps, kbuf, vbuf, qbuf, mst, lst, ast,
    sbuf, sstat, pbuf, pstat, att, wv, acc, s1, r1, s2, r2,
    xsem, qsem, ksem, wsem, rim_s, rim_r, gate_s, gate_r, k_s, k_r, v_s, v_r,
    q_s, q_r, o_s, o_r, t_s, t_r, a_s, a_r, b_s, b_r,
):
    z = lax.axis_index("ctx")
    me = lax.axis_index("mp")
    core = lax.rem(me, 2)
    chip = me // 2
    chips = m // 2
    partner = chip * 2 + 1 - core
    pivot = n // 3
    slots = n - pivot
    rows = xb.shape[1]
    heads = gown.shape[0]
    groups = lf_ref.shape[0]
    per_tile = groups // heads
    width = HD // per_tile
    tap_count = lf_ref.shape[1]
    short = sf_ref.shape[0]
    span = min(3, slots) * rows
    query_groups = qbuf.shape[1] // span
    cols = out_ref.shape[1]
    channels = xb.shape[2]
    own = jnp.minimum(z, pivot)

    def remote(src, dst, ss, rs, axis, target):
        return pltpu.make_async_remote_copy(
            src_ref=src, dst_ref=dst, send_sem=ss, recv_sem=rs,
            device_id={axis: target}, device_id_type=MESH)

    local_x = pltpu.make_async_copy(x_hbm, xb, xsem)
    local_x.start()
    local_k, local_q = [], []
    for h in range(heads):
        part = pl.ds(h * HD, HD)
        local_k.append(pltpu.make_async_copy(k_hbm.at[:, part], kbuf.at[own, h], ksem.at[h]))
        local_q.append(pltpu.make_async_copy(q_hbm.at[:, part], qbuf.at[h, pl.ds(0, rows)], qsem.at[h]))
    for c in local_k + local_q:
        c.start()
    local_w = pltpu.make_async_copy(w_hbm, wv, wsem)
    local_w.start()

    barrier = pltpu.get_barrier_semaphore()
    count = jnp.int32(m - 1)
    for other in range(m):
        @pl.when(other != me)
        def _():
            pl.semaphore_signal(barrier, inc=1, device_id={"mp": other}, device_id_type=MESH)
    for other in range(n):
        low, high = jnp.minimum(z, other), jnp.maximum(z, other)
        talks = (low != high) & ((high == low + 1) | (high <= pivot) | (low >= pivot))
        count = count + talks.astype(jnp.int32)

        @pl.when(talks)
        def _():
            pl.semaphore_signal(barrier, inc=1, device_id={"ctx": other}, device_id_type=MESH)

    local_x.wait()
    for j in range(3):
        rim_out[2 * j:2 * j + 2, :] = xb[j, rows - 2:rows, :]

    @pl.when(z == 0)
    def _():
        rim_in[...] = jnp.zeros_like(rim_in)
        gprev[...] = jnp.zeros_like(gprev)

    pl.semaphore_wait(barrier, count)

    up = jnp.minimum(z + 1, n - 1)
    rim = remote(rim_out, rim_in, rim_s, rim_r, "ctx", up)

    def gate(h):
        return remote(gown.at[h], gprev.at[h], gate_s.at[h], gate_r.at[h], "ctx", up)

    @pl.when(z < n - 1)
    def _():
        rim.start()

    for c in local_k + local_q:
        c.wait()

    def each_query(h, act):
        for other in range(pivot, n - 1):
            @pl.when(other < z)
            def _():
                act(remote(
                    qbuf.at[h, pl.ds(0, rows)],
                    qbuf.at[h, pl.ds(pl.multiple_of((z - other) * rows, rows), rows)],
                    q_s.at[other - pivot, h], q_r.at[z - other, h], "ctx", other))

    def each_key(h, act):
        for other in range(1, pivot + 1):
            @pl.when((other > z) & (z < pivot))
            def _():
                act(remote(kbuf.at[own, h], kbuf.at[own, h], k_s.at[other, h], k_r.at[own, h], "ctx", other))

    def each_value(h, act):
        for other in range(1, pivot + 1):
            @pl.when((other > z) & (z < pivot))
            def _():
                act(remote(vbuf.at[own, h], vbuf.at[own, h], v_s.at[other, h], v_r.at[own, h], "ctx", other))

    early = min(2, heads)
    for h in range(early):
        each_key(h, lambda c: c.start())

    @pl.loop(0, heads)
    def _(h):
        each_query(h, lambda c: c.start())

    @pl.when(z > 0)
    def _():
        rim.wait_recv()

    row = lax.broadcasted_iota(jnp.int32, (rows, HD), 0)

    @pl.loop(0, heads)
    def _(h):
        part = pl.ds(pl.multiple_of(h * HD, HD), HD)
        edge = rim_in[:, part].astype(F32)
        feats = []
        for j in range(3):
            x = xb[j, :, part].astype(F32)
            last = edge[2 * j + 1:2 * j + 2]
            x1 = jnp.where(row == 0, last, pltpu.roll(x, 1, 0))
            x2 = jnp.where(row == 0, edge[2 * j:2 * j + 1],
                           jnp.where(row == 1, last, pltpu.roll(x, 2, 0)))
            total = sf_ref[0, j:j + 1, part].astype(F32) * x
            total = total + sf_ref[1, j:j + 1, part].astype(F32) * x1
            feats.append(total + sf_ref[2, j:j + 1, part].astype(F32) * x2)
        f0[h] = feats[0]
        gown[h] = (feats[1] * feats[2]).astype(BF)

        @pl.when(z < n - 1)
        def _():
            gate(h).start()

    flip = (lax.broadcasted_iota(jnp.int32, (tap_count, 2 * rows), 0)
            + lax.broadcasted_iota(jnp.int32, (tap_count, 2 * rows), 1)) == rows
    based = dot(lf_ref[...], flip.astype(BF))
    for g in range(groups):
        wide = jnp.broadcast_to(based[g:g + 1], (rows, 2 * rows))
        taps[g] = pltpu.roll(wide, 0, 1, stride=1, stride_axis=0).astype(BF)
    acc[...] = jnp.zeros_like(acc)

    lane = lax.broadcasted_iota(jnp.int32, (rows, HD), 1) // width

    @pl.loop(0, heads)
    def _(h):
        @pl.when(z > 0)
        def _():
            gate(h).wait_recv()

        mine = gown[h]
        both = jnp.concatenate([gprev[h], mine], axis=0)
        filt = jnp.zeros((rows, HD), F32)
        for g in range(per_tile):
            filt = jnp.where(lane == g, dot(taps[h * per_tile + g], both), filt)
        part = pl.ds(pl.multiple_of(h * HD, HD), HD)
        val = f0[h] * (filt + skip_ref[:, part] * mine.astype(F32))
        vbuf[own, h] = val.T.astype(BF)

        @pl.when(h >= early)
        def _():
            each_key(h, lambda c: c.start())

        each_value(h, lambda c: c.start())

    scale = HD ** -0.5
    krow = lax.broadcasted_iota(jnp.int32, (rows, span), 0)
    kcol = lax.broadcasted_iota(jnp.int32, (rows, span), 1)

    def each_part(h, act):
        for s in range(1, slots):
            @pl.when((z >= pivot) & (z + s < n))
            def _():
                act(s,
                    remote(sbuf.at[s - 1, h], pbuf.at[z - pivot, h],
                           o_s.at[s - 1, h], o_r.at[z - pivot, h], "ctx", z + s),
                    remote(sstat.at[s - 1, h], pstat.at[z - pivot, h],
                           t_s.at[s - 1, h], t_r.at[z - pivot, h], "ctx", z + s))

    def hand_over(h):
        def act(s, o, t):
            gi, at = (s * rows) // span, (s * rows) % span
            mm = mst[h, gi, :, at:at + rows]
            ll = lst[h, gi, :, at:at + rows]
            aa = ast[h, gi, :, at:at + rows]
            sbuf[s - 1, h] = (aa * (1.0 / ll[0:1])).astype(BF)
            sstat[s - 1, h] = mm + jnp.log(ll)
            o.start()
            t.start()
        each_part(h, act)

    def own_keys(h):
        for s in range(1, slots):
            @pl.when((z >= pivot) & (z + s < n))
            def _():
                remote(qbuf.at[h, pl.ds(0, rows)], qbuf.at[h, pl.ds(s * rows, rows)],
                       q_s.at[0, h], q_r.at[s, h], "ctx", jnp.minimum(z + s, n - 1)).wait_recv()

        for gi in range(query_groups):
            q = qbuf[h, gi * span:(gi + 1) * span]
            s = dot(kbuf[own, h], q, 1, 1) * scale
            s = jnp.where(krow <= kcol + gi * span, s, NEG)
            mx = jnp.max(s, axis=0, keepdims=True)
            p = jnp.exp(s - mx)
            mst[h, gi] = jnp.broadcast_to(mx, (8, span))
            lst[h, gi] = jnp.broadcast_to(jnp.sum(p, axis=0, keepdims=True), (8, span))
            ast[h, gi] = dot(vbuf[own, h], p.astype(BF))

    @pl.when(z > pivot)
    def _():
        @pl.loop(0, heads)
        def _(h):
            own_keys(h)
            hand_over(h)

    def one_head(h):
        @pl.when(z <= pivot)
        def _():
            own_keys(h)

        @pl.loop(0, jnp.where(z <= pivot, z, 0))
        def _(j):
            remote(kbuf.at[j, h], kbuf.at[j, h], k_s.at[0, 0], k_r.at[j, h], "ctx", j).wait_recv()
            remote(vbuf.at[j, h], vbuf.at[j, h], v_s.at[0, 0], v_r.at[j, h], "ctx", j).wait_recv()
            for gi in range(query_groups):
                q = qbuf[h, gi * span:(gi + 1) * span]
                s = dot(kbuf[j, h], q, 1, 1) * scale
                old = mst[h, gi, 0:1]
                mx = jnp.maximum(old, jnp.max(s, axis=0, keepdims=True))
                p = jnp.exp(s - mx)
                fade = jnp.exp(old - mx)
                mst[h, gi] = jnp.broadcast_to(mx, (8, span))
                lst[h, gi] = jnp.broadcast_to(
                    lst[h, gi, 0:1] * fade + jnp.sum(p, axis=0, keepdims=True), (8, span))
                ast[h, gi] = ast[h, gi] * fade + dot(vbuf[j, h], p.astype(BF))

        @pl.when(z == pivot)
        def _():
            hand_over(h)

        @pl.loop(0, jnp.maximum(z - pivot, 0))
        def _(j):
            remote(sbuf.at[0, 0], pbuf.at[j, h], o_s.at[0, 0], o_r.at[j, h], "ctx", j + pivot).wait_recv()
            remote(sstat.at[0, 0], pstat.at[j, h], t_s.at[0, 0], t_r.at[j, h], "ctx", j + pivot).wait_recv()
            old = mst[h, 0, :, 0:rows]
            lse = pstat[j, h]
            mx = jnp.maximum(old, lse)
            fade, gain = jnp.exp(old - mx), jnp.exp(lse - mx)
            mst[h, 0, :, 0:rows] = mx
            lst[h, 0, :, 0:rows] = lst[h, 0, :, 0:rows] * fade + gain
            ast[h, 0, :, 0:rows] = ast[h, 0, :, 0:rows] * fade[0:1] + pbuf[j, h].astype(F32) * gain[0:1]

        done = ast[h, 0, :, 0:rows] * (1.0 / lst[h, 0, 0:1, 0:rows])
        return done.T.astype(BF)

    @pl.loop(0, heads // 2)
    def _(c):
        att[c, :, 0:HD] = one_head(2 * c)
        att[c, :, HD:2 * HD] = one_head(2 * c + 1)

        @pl.when(c == 0)
        def _():
            local_w.wait()

        @pl.when(c < heads // 2 - 1)
        def _():
            lhs = att[c]

            @pl.loop(0, m)
            def _(b):
                at = pl.ds(pl.multiple_of(b * cols, cols), cols)
                acc[b] += dot(lhs, wv[pl.ds(pl.multiple_of(c * 2 * HD, 2 * HD), 2 * HD), at])

    pieces = 4
    piece = cols // pieces

    def across(d, i):
        return remote(s1.at[d, i], r1.at[d, i], a_s.at[d, i], a_r.at[d, i], "mp", partner)

    def along(d, i):
        there = lax.rem(chip + d, chips) * 2 + core
        return remote(s2.at[d, i], r2.at[d, i], b_s.at[d, i], b_r.at[d, i], "mp", there)

    last = att[heads // 2 - 1]

    def summed(b, i):
        at = pl.ds(pl.multiple_of(b * cols + i * piece, piece), piece)
        return acc[b, :, i * piece:(i + 1) * piece] + dot(last, wv[channels - 2 * HD:, at])

    def block(d, side):
        return lax.rem(chip + d, chips) * 2 + side

    order = [d % chips for d in range(1, chips + 1)]
    for d in order:
        for i in range(pieces):
            s1[d, i] = summed(block(d, 1 - core), i).astype(BF)
            across(d, i).start()
    for d in range(1, chips):
        for i in range(pieces):
            total = summed(block(d, core), i)
            across(d, i).wait_recv()
            s2[d, i] = (total + r1[d, i].astype(F32)).astype(BF)
            along(d, i).start()
    for i in range(pieces):
        acc[me, :, i * piece:(i + 1) * piece] = summed(me, i)
    for i in range(pieces):
        across(0, i).wait_recv()
        acc[me, :, i * piece:(i + 1) * piece] += r1[0, i].astype(F32)
    for i in range(pieces):
        total = acc[me, :, i * piece:(i + 1) * piece]
        for d in range(1, chips):
            along(d, i).wait_recv()
            total = total + r2[d, i].astype(F32)
        out_ref[:, i * piece:(i + 1) * piece] = total.astype(BF)

    for i in range(pieces):
        for d in range(chips):
            across(d, i).wait_send()
        for d in range(1, chips):
            along(d, i).wait_send()

    @pl.when(z < n - 1)
    def _():
        rim.wait_send()

    @pl.loop(0, heads)
    def _(h):
        def ended(s, o, t):
            o.wait_send()
            t.wait_send()
        @pl.when(z < n - 1)
        def _():
            gate(h).wait_send()

        each_query(h, lambda c: c.wait_send())
        each_key(h, lambda c: c.wait_send())
        each_value(h, lambda c: c.wait_send())
        each_part(h, ended)


def per_device(n, m, inputs, short_filter, long_filter, skip_gain, queries, key_rows, out_weight):
    rows, _, channels = inputs.shape
    heads = channels // HD
    groups = long_filter.shape[0]
    total = out_weight.shape[1]
    cols = total // m
    chips = m // 2
    pivot = n // 3
    slots = n - pivot
    batch = min(3, slots)
    padded = -(-slots // batch) * batch
    span = batch * rows
    gq = padded // batch
    parts = max(slots - 1, 1)
    vm = pltpu.VMEM
    dma = pltpu.SemaphoreType.DMA
    scratch = [
        vm((3, rows, channels), BF), vm((16, channels), BF), vm((16, channels), BF),
        vm((heads, rows, HD), F32), vm((heads, rows, HD), BF), vm((heads, rows, HD), BF),
        vm((groups, rows, 2 * rows), BF),
        vm((pivot + 1, heads, rows, HD), BF), vm((pivot + 1, heads, HD, rows), BF),
        vm((heads, padded * rows, HD), BF),
        vm((heads, gq, 8, span), F32), vm((heads, gq, 8, span), F32), vm((heads, gq, HD, span), F32),
        vm((parts, heads, HD, rows), BF), vm((parts, heads, 8, rows), F32),
        vm((parts, heads, HD, rows), BF), vm((parts, heads, 8, rows), F32),
        vm((heads // 2, rows, 2 * HD), BF), vm((channels, total), BF), vm((m, rows, cols), F32),
    ] + [vm((chips, 4, rows, cols // 4), BF)] * 4 + [
        dma, dma((heads,)), dma((heads,)), dma, dma, dma, dma((heads,)), dma((heads,)),
    ] + [dma((pivot + 1, heads))] * 4 + [dma((slots, heads))] * 2 + [
        dma((parts, heads)), dma((parts, heads)), dma((parts, heads)), dma((parts, heads)),
    ] + [dma((chips, 4))] * 4
    in_vmem = pl.BlockSpec(memory_space=pltpu.VMEM)
    in_hbm = pl.BlockSpec(memory_space=pl.ANY)
    return pl.pallas_call(
        functools.partial(kernel, n, m),
        out_shape=jax.ShapeDtypeStruct((rows, cols), BF),
        in_specs=[in_hbm, in_vmem, in_vmem, in_vmem, in_hbm, in_hbm, in_hbm],
        out_specs=in_vmem,
        scratch_shapes=scratch,
        compiler_params=pltpu.CompilerParams(
            collective_id=0, has_side_effects=True, vmem_limit_bytes=60 * 2**20),
    )(inputs.transpose(1, 0, 2), short_filter, long_filter, skip_gain[None], queries, key_rows, out_weight)


def solution(mesh):
    placed = (
        P(("parts", "ctx"), None, "mp"),
        P(None, None, "mp"),
        P("mp", None),
        P("mp"),
        P(("parts", "ctx"), "mp"),
        P(("parts", "ctx"), "mp"),
        P("mp", None),
    )
    return jax.shard_map(
        functools.partial(per_device, mesh.shape["ctx"], mesh.shape["mp"]),
        mesh=mesh, in_specs=placed, out_specs=P(("parts", "ctx"), "mp"), check_vma=False)
```

```python
import functools

import jax
import jax.numpy as jnp
from jax import lax
from jax.experimental import pallas as pl
from jax.experimental.pallas import tpu as pltpu
from jax.sharding import PartitionSpec as P

HD = 128
MESH = pl.DeviceIdType.MESH
NEG = -1e30
F32 = jnp.float32
BF = jnp.bfloat16


def dot(a, b, ca=1, cb=0):
    return lax.dot_general(a, b, (((ca,), (cb,)), ((), ())), preferred_element_type=F32)


def kernel(
    n, m, x_hbm, sf_hbm, lf_hbm, skip_hbm, q_hbm, k_hbm, w_hbm, out_ref,
    sf_ref, lf_ref, skip_ref, psem, xb, rim_out, rim_in, f0, gown, gprev, taps, kbuf, vbuf, qbuf, mst, lst, ast,
    sbuf, sstat, pbuf, pstat, att, wv, acc, s1, r1, s2, r2,
    xsem, qsem, ksem, wsem, rim_s, rim_r, gate_s, gate_r, k_s, k_r, v_s, v_r,
    q_s, q_r, o_s, o_r, t_s, t_r, a_s, a_r, b_s, b_r,
):
    z = lax.axis_index("ctx")
    me = lax.axis_index("mp")
    core = lax.rem(me, 2)
    chip = me // 2
    chips = m // 2
    partner = chip * 2 + 1 - core
    pivot = n // 3
    slots = n - pivot
    rows = xb.shape[1]
    heads = gown.shape[0]
    groups = lf_ref.shape[0]
    per_tile = groups // heads
    width = HD // per_tile
    tap_count = lf_ref.shape[1]
    short = sf_ref.shape[0]
    span = min(3, slots) * rows
    query_groups = qbuf.shape[1] // span
    cols = out_ref.shape[1]
    channels = xb.shape[2]
    own = jnp.minimum(z, pivot)

    def remote(src, dst, ss, rs, axis, target):
        return pltpu.make_async_remote_copy(
            src_ref=src, dst_ref=dst, send_sem=ss, recv_sem=rs,
            device_id={axis: target}, device_id_type=MESH)

    barrier = pltpu.get_barrier_semaphore()
    count = jnp.int32(m - 1)
    for other in range(m):
        @pl.when(other != me)
        def _():
            pl.semaphore_signal(barrier, inc=1, device_id={"mp": other}, device_id_type=MESH)
    for other in range(n):
        low, high = jnp.minimum(z, other), jnp.maximum(z, other)
        talks = (low != high) & ((high == low + 1) | (high <= pivot) | (low >= pivot))
        count = count + talks.astype(jnp.int32)

        @pl.when(talks)
        def _():
            pl.semaphore_signal(barrier, inc=1, device_id={"ctx": other}, device_id_type=MESH)

    local_x = pltpu.make_async_copy(x_hbm, xb, xsem)
    local_x.start()
    small = [pltpu.make_async_copy(a, b, psem.at[i]) for i, (a, b) in enumerate(
        ((sf_hbm, sf_ref), (lf_hbm, lf_ref), (skip_hbm, skip_ref)))]
    for c in small:
        c.start()
    local_k, local_q = [], []
    for h in range(heads):
        part = pl.ds(h * HD, HD)
        local_k.append(pltpu.make_async_copy(k_hbm.at[:, part], kbuf.at[own, h], ksem.at[h]))
        local_q.append(pltpu.make_async_copy(q_hbm.at[:, part], qbuf.at[h, pl.ds(0, rows)], qsem.at[h]))
    for c in local_k + local_q:
        c.start()
    local_w = pltpu.make_async_copy(w_hbm, wv, wsem)
    local_w.start()

    local_x.wait()
    for j in range(3):
        rim_out[2 * j:2 * j + 2, :] = xb[j, rows - 2:rows, :]

    @pl.when(z == 0)
    def _():
        rim_in[...] = jnp.zeros_like(rim_in)
        gprev[...] = jnp.zeros_like(gprev)

    pl.semaphore_wait(barrier, count)

    up = jnp.minimum(z + 1, n - 1)
    rim = remote(rim_out, rim_in, rim_s, rim_r, "ctx", up)

    def gate(h):
        return remote(gown.at[h], gprev.at[h], gate_s.at[h], gate_r.at[h], "ctx", up)

    @pl.when(z < n - 1)
    def _():
        rim.start()

    for c in local_k + local_q:
        c.wait()

    def each_query(h, act):
        for other in range(pivot, n - 1):
            @pl.when(other < z)
            def _():
                act(remote(
                    qbuf.at[h, pl.ds(0, rows)],
                    qbuf.at[h, pl.ds(pl.multiple_of((z - other) * rows, rows), rows)],
                    q_s.at[other - pivot, h], q_r.at[z - other, h], "ctx", other))

    def each_key(h, act):
        for other in range(1, pivot + 1):
            @pl.when((other > z) & (z < pivot))
            def _():
                act(remote(kbuf.at[own, h], kbuf.at[own, h], k_s.at[other, h], k_r.at[own, h], "ctx", other))

    def each_value(h, act):
        for other in range(1, pivot + 1):
            @pl.when((other > z) & (z < pivot))
            def _():
                act(remote(vbuf.at[own, h], vbuf.at[own, h], v_s.at[other, h], v_r.at[own, h], "ctx", other))

    early = min(2, heads)
    for h in range(early):
        each_key(h, lambda c: c.start())

    @pl.loop(0, heads)
    def _(h):
        each_query(h, lambda c: c.start())

    @pl.when(z > 0)
    def _():
        rim.wait_recv()

    for c in small:
        c.wait()
    row = lax.broadcasted_iota(jnp.int32, (rows, HD), 0)

    @pl.loop(0, heads)
    def _(h):
        part = pl.ds(pl.multiple_of(h * HD, HD), HD)
        edge = rim_in[:, part].astype(F32)
        feats = []
        for j in range(3):
            x = xb[j, :, part].astype(F32)
            last = edge[2 * j + 1:2 * j + 2]
            x1 = jnp.where(row == 0, last, pltpu.roll(x, 1, 0))
            x2 = jnp.where(row == 0, edge[2 * j:2 * j + 1],
                           jnp.where(row == 1, last, pltpu.roll(x, 2, 0)))
            total = sf_ref[0, j:j + 1, part].astype(F32) * x
            total = total + sf_ref[1, j:j + 1, part].astype(F32) * x1
            feats.append(total + sf_ref[2, j:j + 1, part].astype(F32) * x2)
        f0[h] = feats[0]
        gown[h] = (feats[1] * feats[2]).astype(BF)

        @pl.when(z < n - 1)
        def _():
            gate(h).start()

    flip = (lax.broadcasted_iota(jnp.int32, (tap_count, 2 * rows), 0)
            + lax.broadcasted_iota(jnp.int32, (tap_count, 2 * rows), 1)) == rows
    based = dot(lf_ref[...], flip.astype(BF))
    for g in range(groups):
        wide = jnp.broadcast_to(based[g:g + 1], (rows, 2 * rows))
        taps[g] = pltpu.roll(wide, 0, 1, stride=1, stride_axis=0).astype(BF)
    acc[...] = jnp.zeros_like(acc)

    lane = lax.broadcasted_iota(jnp.int32, (rows, HD), 1) // width

    @pl.loop(0, heads)
    def _(h):
        @pl.when(z > 0)
        def _():
            gate(h).wait_recv()

        mine = gown[h]
        both = jnp.concatenate([gprev[h], mine], axis=0)
        filt = jnp.zeros((rows, HD), F32)
        for g in range(per_tile):
            filt = jnp.where(lane == g, dot(taps[h * per_tile + g], both), filt)
        part = pl.ds(pl.multiple_of(h * HD, HD), HD)
        val = f0[h] * (filt + skip_ref[:, part] * mine.astype(F32))
        vbuf[own, h] = val.T.astype(BF)

        @pl.when(h >= early)
        def _():
            each_key(h, lambda c: c.start())

        each_value(h, lambda c: c.start())

    scale = HD ** -0.5
    krow = lax.broadcasted_iota(jnp.int32, (rows, span), 0)
    kcol = lax.broadcasted_iota(jnp.int32, (rows, span), 1)

    def each_part(h, act):
        for s in range(1, slots):
            @pl.when((z >= pivot) & (z + s < n))
            def _():
                act(s,
                    remote(sbuf.at[s - 1, h], pbuf.at[z - pivot, h],
                           o_s.at[s - 1, h], o_r.at[z - pivot, h], "ctx", z + s),
                    remote(sstat.at[s - 1, h], pstat.at[z - pivot, h],
                           t_s.at[s - 1, h], t_r.at[z - pivot, h], "ctx", z + s))

    def hand_over(h):
        def act(s, o, t):
            gi, at = (s * rows) // span, (s * rows) % span
            mm = mst[h, gi, :, at:at + rows]
            ll = lst[h, gi, :, at:at + rows]
            aa = ast[h, gi, :, at:at + rows]
            sbuf[s - 1, h] = (aa * (1.0 / ll[0:1])).astype(BF)
            sstat[s - 1, h] = mm + jnp.log(ll)
            o.start()
            t.start()
        each_part(h, act)

    def own_keys(h):
        for s in range(1, slots):
            @pl.when((z >= pivot) & (z + s < n))
            def _():
                remote(qbuf.at[h, pl.ds(0, rows)], qbuf.at[h, pl.ds(s * rows, rows)],
                       q_s.at[0, h], q_r.at[s, h], "ctx", jnp.minimum(z + s, n - 1)).wait_recv()

        for gi in range(query_groups):
            q = qbuf[h, gi * span:(gi + 1) * span]
            s = dot(kbuf[own, h], q, 1, 1) * scale
            s = jnp.where(krow <= kcol + gi * span, s, NEG)
            mx = jnp.max(s, axis=0, keepdims=True)
            p = jnp.exp(s - mx)
            mst[h, gi] = jnp.broadcast_to(mx, (8, span))
            lst[h, gi] = jnp.broadcast_to(jnp.sum(p, axis=0, keepdims=True), (8, span))
            ast[h, gi] = dot(vbuf[own, h], p.astype(BF))

    @pl.when(z > pivot)
    def _():
        @pl.loop(0, heads)
        def _(h):
            own_keys(h)
            hand_over(h)

    def one_head(h):
        @pl.when(z <= pivot)
        def _():
            own_keys(h)

        @pl.loop(0, jnp.where(z <= pivot, z, 0))
        def _(j):
            remote(kbuf.at[j, h], kbuf.at[j, h], k_s.at[0, 0], k_r.at[j, h], "ctx", j).wait_recv()
            remote(vbuf.at[j, h], vbuf.at[j, h], v_s.at[0, 0], v_r.at[j, h], "ctx", j).wait_recv()
            for gi in range(query_groups):
                q = qbuf[h, gi * span:(gi + 1) * span]
                s = dot(kbuf[j, h], q, 1, 1) * scale
                old = mst[h, gi, 0:1]
                mx = jnp.maximum(old, jnp.max(s, axis=0, keepdims=True))
                p = jnp.exp(s - mx)
                fade = jnp.exp(old - mx)
                mst[h, gi] = jnp.broadcast_to(mx, (8, span))
                lst[h, gi] = jnp.broadcast_to(
                    lst[h, gi, 0:1] * fade + jnp.sum(p, axis=0, keepdims=True), (8, span))
                ast[h, gi] = ast[h, gi] * fade + dot(vbuf[j, h], p.astype(BF))

        @pl.when(z == pivot)
        def _():
            hand_over(h)

        @pl.loop(0, jnp.maximum(z - pivot, 0))
        def _(j):
            remote(sbuf.at[0, 0], pbuf.at[j, h], o_s.at[0, 0], o_r.at[j, h], "ctx", j + pivot).wait_recv()
            remote(sstat.at[0, 0], pstat.at[j, h], t_s.at[0, 0], t_r.at[j, h], "ctx", j + pivot).wait_recv()
            old = mst[h, 0, :, 0:rows]
            lse = pstat[j, h]
            mx = jnp.maximum(old, lse)
            fade, gain = jnp.exp(old - mx), jnp.exp(lse - mx)
            mst[h, 0, :, 0:rows] = mx
            lst[h, 0, :, 0:rows] = lst[h, 0, :, 0:rows] * fade + gain
            ast[h, 0, :, 0:rows] = ast[h, 0, :, 0:rows] * fade[0:1] + pbuf[j, h].astype(F32) * gain[0:1]

        done = ast[h, 0, :, 0:rows] * (1.0 / lst[h, 0, 0:1, 0:rows])
        return done.T.astype(BF)

    @pl.loop(0, heads // 2)
    def _(c):
        att[c, :, 0:HD] = one_head(2 * c)
        att[c, :, HD:2 * HD] = one_head(2 * c + 1)

        @pl.when(c == 0)
        def _():
            local_w.wait()

        @pl.when(c < heads // 2 - 1)
        def _():
            lhs = att[c]

            @pl.loop(0, m)
            def _(b):
                at = pl.ds(pl.multiple_of(b * cols, cols), cols)
                acc[b] += dot(lhs, wv[pl.ds(pl.multiple_of(c * 2 * HD, 2 * HD), 2 * HD), at])

    pieces = 4
    piece = cols // pieces

    def across(d, i):
        return remote(s1.at[d, i], r1.at[d, i], a_s.at[d, i], a_r.at[d, i], "mp", partner)

    def along(d, i):
        there = lax.rem(chip + d, chips) * 2 + core
        return remote(s2.at[d, i], r2.at[d, i], b_s.at[d, i], b_r.at[d, i], "mp", there)

    last = att[heads // 2 - 1]

    def summed(b, i):
        at = pl.ds(pl.multiple_of(b * cols + i * piece, piece), piece)
        return acc[b, :, i * piece:(i + 1) * piece] + dot(last, wv[channels - 2 * HD:, at])

    def block(d, side):
        return lax.rem(chip + d, chips) * 2 + side

    order = [d % chips for d in range(1, chips + 1)]
    for d in order:
        for i in range(pieces):
            s1[d, i] = summed(block(d, 1 - core), i).astype(BF)
            across(d, i).start()
    for d in range(1, chips):
        for i in range(pieces):
            total = summed(block(d, core), i)
            across(d, i).wait_recv()
            s2[d, i] = (total + r1[d, i].astype(F32)).astype(BF)
            along(d, i).start()
    for i in range(pieces):
        acc[me, :, i * piece:(i + 1) * piece] = summed(me, i)
    for i in range(pieces):
        across(0, i).wait_recv()
        acc[me, :, i * piece:(i + 1) * piece] += r1[0, i].astype(F32)
    for i in range(pieces):
        total = acc[me, :, i * piece:(i + 1) * piece]
        for d in range(1, chips):
            along(d, i).wait_recv()
            total = total + r2[d, i].astype(F32)
        out_ref[:, i * piece:(i + 1) * piece] = total.astype(BF)

    for i in range(pieces):
        for d in range(chips):
            across(d, i).wait_send()
        for d in range(1, chips):
            along(d, i).wait_send()

    @pl.when(z < n - 1)
    def _():
        rim.wait_send()

    @pl.loop(0, heads)
    def _(h):
        def ended(s, o, t):
            o.wait_send()
            t.wait_send()
        @pl.when(z < n - 1)
        def _():
            gate(h).wait_send()

        each_query(h, lambda c: c.wait_send())
        each_key(h, lambda c: c.wait_send())
        each_value(h, lambda c: c.wait_send())
        each_part(h, ended)


def per_device(n, m, inputs, short_filter, long_filter, skip_gain, queries, key_rows, out_weight):
    rows, _, channels = inputs.shape
    heads = channels // HD
    groups = long_filter.shape[0]
    total = out_weight.shape[1]
    cols = total // m
    chips = m // 2
    pivot = n // 3
    slots = n - pivot
    batch = min(3, slots)
    padded = -(-slots // batch) * batch
    span = batch * rows
    gq = padded // batch
    parts = max(slots - 1, 1)
    vm = pltpu.VMEM
    dma = pltpu.SemaphoreType.DMA
    scratch = [
        vm(short_filter.shape, BF), vm(long_filter.shape, BF), vm((1, channels), F32), dma((3,)),
        vm((3, rows, channels), BF), vm((16, channels), BF), vm((16, channels), BF),
        vm((heads, rows, HD), F32), vm((heads, rows, HD), BF), vm((heads, rows, HD), BF),
        vm((groups, rows, 2 * rows), BF),
        vm((pivot + 1, heads, rows, HD), BF), vm((pivot + 1, heads, HD, rows), BF),
        vm((heads, padded * rows, HD), BF),
        vm((heads, gq, 8, span), F32), vm((heads, gq, 8, span), F32), vm((heads, gq, HD, span), F32),
        vm((parts, heads, HD, rows), BF), vm((parts, heads, 8, rows), F32),
        vm((parts, heads, HD, rows), BF), vm((parts, heads, 8, rows), F32),
        vm((heads // 2, rows, 2 * HD), BF), vm((channels, total), BF), vm((m, rows, cols), F32),
    ] + [vm((chips, 4, rows, cols // 4), BF)] * 4 + [
        dma, dma((heads,)), dma((heads,)), dma, dma, dma, dma((heads,)), dma((heads,)),
    ] + [dma((pivot + 1, heads))] * 4 + [dma((slots, heads))] * 2 + [
        dma((parts, heads)), dma((parts, heads)), dma((parts, heads)), dma((parts, heads)),
    ] + [dma((chips, 4))] * 4
    in_vmem = pl.BlockSpec(memory_space=pltpu.VMEM)
    in_hbm = pl.BlockSpec(memory_space=pl.ANY)
    return pl.pallas_call(
        functools.partial(kernel, n, m),
        out_shape=pltpu.VMEM((rows, cols), BF),
        in_specs=[in_hbm] * 7,
        out_specs=in_vmem,
        scratch_shapes=scratch,
        compiler_params=pltpu.CompilerParams(
            collective_id=0, has_side_effects=True, vmem_limit_bytes=60 * 2**20),
    )(inputs.transpose(1, 0, 2), short_filter, long_filter, skip_gain[None], queries, key_rows, out_weight)


def solution(mesh):
    placed = (
        P(("parts", "ctx"), None, "mp"),
        P(None, None, "mp"),
        P("mp", None),
        P("mp"),
        P(("parts", "ctx"), "mp"),
        P(("parts", "ctx"), "mp"),
        P("mp", None),
    )
    return jax.shard_map(
        functools.partial(per_device, mesh.shape["ctx"], mesh.shape["mp"]),
        mesh=mesh, in_specs=placed, out_specs=P(("parts", "ctx"), "mp"), check_vma=False)
```

```python
import functools

import jax
import jax.numpy as jnp
from jax import lax
from jax.experimental import pallas as pl
from jax.experimental.pallas import tpu as pltpu
from jax.sharding import PartitionSpec as P

HD = 128
MESH = pl.DeviceIdType.MESH
NEG = -1e30
F32 = jnp.float32
BF = jnp.bfloat16


def dot(a, b, ca=1, cb=0):
    return lax.dot_general(a, b, (((ca,), (cb,)), ((), ())), preferred_element_type=F32)


def kernel(
    n, m, x_hbm, sf_hbm, lf_hbm, skip_hbm, q_hbm, k_hbm, w_hbm, out_ref,
    sf_ref, lf_ref, skip_ref, psem, xb, rim_out, rim_in, f0, gown, gprev, taps, kbuf, vbuf, qbuf, mst, lst, ast,
    sbuf, sstat, pbuf, pstat, att, wv, acc, s1, r1, s2, r2,
    xsem, qsem, ksem, wsem, rim_s, rim_r, gate_s, gate_r, k_s, k_r, v_s, v_r,
    q_s, q_r, o_s, o_r, t_s, t_r, a_s, a_r, b_s, b_r,
):
    z = lax.axis_index("ctx")
    me = lax.axis_index("mp")
    core = lax.rem(me, 2)
    chip = me // 2
    chips = m // 2
    partner = chip * 2 + 1 - core
    pivot = n // 3
    slots = n - pivot
    rows = xb.shape[1]
    heads = gown.shape[0]
    groups = lf_ref.shape[0]
    per_tile = groups // heads
    width = HD // per_tile
    tap_count = lf_ref.shape[1]
    short = sf_ref.shape[0]
    span = min(3, slots) * rows
    query_groups = qbuf.shape[1] // span
    cols = out_ref.shape[1]
    channels = xb.shape[2]
    own = jnp.minimum(z, pivot)

    def remote(src, dst, ss, rs, axis, target):
        return pltpu.make_async_remote_copy(
            src_ref=src, dst_ref=dst, send_sem=ss, recv_sem=rs,
            device_id={axis: target}, device_id_type=MESH)

    barrier = pltpu.get_barrier_semaphore()
    count = jnp.int32(m - 1)
    for other in range(m):
        @pl.when(other != me)
        def _():
            pl.semaphore_signal(barrier, inc=1, device_id={"mp": other}, device_id_type=MESH)
    for other in range(n):
        low, high = jnp.minimum(z, other), jnp.maximum(z, other)
        talks = (low != high) & ((high == low + 1) | (high <= pivot) | (low >= pivot))
        count = count + talks.astype(jnp.int32)

        @pl.when(talks)
        def _():
            pl.semaphore_signal(barrier, inc=1, device_id={"ctx": other}, device_id_type=MESH)

    local_x = pltpu.make_async_copy(x_hbm, xb, xsem)
    local_x.start()
    small = [pltpu.make_async_copy(a, b, psem.at[i]) for i, (a, b) in enumerate(
        ((sf_hbm, sf_ref), (lf_hbm, lf_ref), (skip_hbm, skip_ref)))]
    for c in small:
        c.start()
    local_k, local_q = [], []
    for h in range(heads):
        part = pl.ds(h * HD, HD)
        local_k.append(pltpu.make_async_copy(k_hbm.at[:, part], kbuf.at[own, h], ksem.at[h]))
        local_q.append(pltpu.make_async_copy(q_hbm.at[:, part], qbuf.at[h, pl.ds(0, rows)], qsem.at[h]))
    for c in local_k + local_q:
        c.start()
    local_w = pltpu.make_async_copy(w_hbm, wv, wsem)
    local_w.start()

    local_x.wait()
    for j in range(3):
        rim_out[2 * j:2 * j + 2, :] = xb[j, rows - 2:rows, :]

    @pl.when(z == 0)
    def _():
        rim_in[...] = jnp.zeros_like(rim_in)
        gprev[...] = jnp.zeros_like(gprev)

    pl.semaphore_wait(barrier, count)

    up = jnp.minimum(z + 1, n - 1)
    rim = remote(rim_out, rim_in, rim_s, rim_r, "ctx", up)

    def gate(h):
        return remote(gown.at[h], gprev.at[h], gate_s.at[h], gate_r.at[h], "ctx", up)

    @pl.when(z < n - 1)
    def _():
        rim.start()

    for c in local_k + local_q:
        c.wait()

    def each_query(h, act):
        for other in range(pivot, n - 1):
            @pl.when(other < z)
            def _():
                act(remote(
                    qbuf.at[h, pl.ds(0, rows)],
                    qbuf.at[h, pl.ds(pl.multiple_of((z - other) * rows, rows), rows)],
                    q_s.at[other - pivot, h], q_r.at[z - other, h], "ctx", other))

    def each_key(h, act):
        for other in range(1, pivot + 1):
            @pl.when((other > z) & (z < pivot))
            def _():
                act(remote(kbuf.at[own, h], kbuf.at[own, h], k_s.at[other, h], k_r.at[own, h], "ctx", other))

    def each_value(h, act):
        for other in range(1, pivot + 1):
            @pl.when((other > z) & (z < pivot))
            def _():
                act(remote(vbuf.at[own, h], vbuf.at[own, h], v_s.at[other, h], v_r.at[own, h], "ctx", other))

    early = min(2, heads)
    ahead = min(4, heads)
    for h in range(early):
        each_key(h, lambda c: c.start())

    @pl.loop(0, heads)
    def _(h):
        each_query(h, lambda c: c.start())

    @pl.when(z > 0)
    def _():
        rim.wait_recv()

    for c in small:
        c.wait()
    row = lax.broadcasted_iota(jnp.int32, (rows, HD), 0)

    @pl.loop(0, heads)
    def _(h):
        part = pl.ds(pl.multiple_of(h * HD, HD), HD)
        edge = rim_in[:, part].astype(F32)
        feats = []
        for j in range(3):
            x = xb[j, :, part].astype(F32)
            last = edge[2 * j + 1:2 * j + 2]
            x1 = jnp.where(row == 0, last, pltpu.roll(x, 1, 0))
            x2 = jnp.where(row == 0, edge[2 * j:2 * j + 1],
                           jnp.where(row == 1, last, pltpu.roll(x, 2, 0)))
            total = sf_ref[0, j:j + 1, part].astype(F32) * x
            total = total + sf_ref[1, j:j + 1, part].astype(F32) * x1
            feats.append(total + sf_ref[2, j:j + 1, part].astype(F32) * x2)
        f0[h] = feats[0]
        gown[h] = (feats[1] * feats[2]).astype(BF)

        @pl.when((z < n - 1) & ((z >= pivot) | (h < ahead)))
        def _():
            gate(h).start()

    flip = (lax.broadcasted_iota(jnp.int32, (tap_count, 2 * rows), 0)
            + lax.broadcasted_iota(jnp.int32, (tap_count, 2 * rows), 1)) == rows
    based = dot(lf_ref[...], flip.astype(BF))
    for g in range(groups):
        wide = jnp.broadcast_to(based[g:g + 1], (rows, 2 * rows))
        taps[g] = pltpu.roll(wide, 0, 1, stride=1, stride_axis=0).astype(BF)
    acc[...] = jnp.zeros_like(acc)

    lane = lax.broadcasted_iota(jnp.int32, (rows, HD), 1) // width

    def mix(h):
        @pl.when((z < pivot) & (h >= ahead))
        def _():
            gate(h).start()

        @pl.when(z > 0)
        def _():
            gate(h).wait_recv()

        mine = gown[h]
        both = jnp.concatenate([gprev[h], mine], axis=0)
        filt = jnp.zeros((rows, HD), F32)
        for g in range(per_tile):
            filt = jnp.where(lane == g, dot(taps[h * per_tile + g], both), filt)
        part = pl.ds(pl.multiple_of(h * HD, HD), HD)
        val = f0[h] * (filt + skip_ref[:, part] * mine.astype(F32))
        vbuf[own, h] = val.T.astype(BF)

        @pl.when(h >= early)
        def _():
            each_key(h, lambda c: c.start())

        each_value(h, lambda c: c.start())

    scale = HD ** -0.5
    krow = lax.broadcasted_iota(jnp.int32, (rows, span), 0)
    kcol = lax.broadcasted_iota(jnp.int32, (rows, span), 1)

    def each_part(h, act):
        for s in range(1, slots):
            @pl.when((z >= pivot) & (z + s < n))
            def _():
                act(s,
                    remote(sbuf.at[s - 1, h], pbuf.at[z - pivot, h],
                           o_s.at[s - 1, h], o_r.at[z - pivot, h], "ctx", z + s),
                    remote(sstat.at[s - 1, h], pstat.at[z - pivot, h],
                           t_s.at[s - 1, h], t_r.at[z - pivot, h], "ctx", z + s))

    def hand_over(h):
        def act(s, o, t):
            gi, at = (s * rows) // span, (s * rows) % span
            mm = mst[h, gi, :, at:at + rows]
            ll = lst[h, gi, :, at:at + rows]
            aa = ast[h, gi, :, at:at + rows]
            sbuf[s - 1, h] = (aa * (1.0 / ll[0:1])).astype(BF)
            sstat[s - 1, h] = mm[0:1] + jnp.log(ll[0:1])
            o.start()
            t.start()
        each_part(h, act)

    def own_keys(h):
        for s in range(1, slots):
            @pl.when((z >= pivot) & (z + s < n))
            def _():
                remote(qbuf.at[h, pl.ds(0, rows)], qbuf.at[h, pl.ds(s * rows, rows)],
                       q_s.at[0, h], q_r.at[s, h], "ctx", jnp.minimum(z + s, n - 1)).wait_recv()

        for gi in range(query_groups):
            q = qbuf[h, gi * span:(gi + 1) * span]
            s = dot(kbuf[own, h], q, 1, 1) * scale
            s = jnp.where(krow <= kcol + gi * span, s, NEG)
            mx = jnp.max(s, axis=0, keepdims=True)
            p = jnp.exp(s - mx)
            mst[h, gi] = jnp.broadcast_to(mx, (8, span))
            lst[h, gi] = jnp.broadcast_to(jnp.sum(p, axis=0, keepdims=True), (8, span))
            ast[h, gi] = dot(vbuf[own, h], p.astype(BF))

    @pl.when(z > pivot)
    def _():
        @pl.loop(0, heads)
        def _(h):
            mix(h)
            own_keys(h)
            hand_over(h)

    def one_head(h):
        @pl.when(z <= pivot)
        def _():
            mix(h)
            own_keys(h)

        @pl.loop(0, jnp.where(z <= pivot, z, 0))
        def _(j):
            remote(kbuf.at[j, h], kbuf.at[j, h], k_s.at[0, 0], k_r.at[j, h], "ctx", j).wait_recv()
            remote(vbuf.at[j, h], vbuf.at[j, h], v_s.at[0, 0], v_r.at[j, h], "ctx", j).wait_recv()
            for gi in range(query_groups):
                q = qbuf[h, gi * span:(gi + 1) * span]
                s = dot(kbuf[j, h], q, 1, 1) * scale
                old = mst[h, gi, 0:1]
                mx = jnp.maximum(old, jnp.max(s, axis=0, keepdims=True))
                p = jnp.exp(s - mx)
                fade = jnp.exp(old - mx)
                mst[h, gi] = jnp.broadcast_to(mx, (8, span))
                lst[h, gi] = jnp.broadcast_to(
                    lst[h, gi, 0:1] * fade + jnp.sum(p, axis=0, keepdims=True), (8, span))
                ast[h, gi] = ast[h, gi] * fade + dot(vbuf[j, h], p.astype(BF))

        @pl.when(z == pivot)
        def _():
            hand_over(h)

        @pl.loop(0, jnp.maximum(z - pivot, 0))
        def _(j):
            remote(sbuf.at[0, 0], pbuf.at[j, h], o_s.at[0, 0], o_r.at[j, h], "ctx", j + pivot).wait_recv()
            remote(sstat.at[0, 0], pstat.at[j, h], t_s.at[0, 0], t_r.at[j, h], "ctx", j + pivot).wait_recv()
            old = mst[h, 0, :, 0:rows]
            lse = pstat[j, h]
            mx = jnp.maximum(old, lse)
            fade, gain = jnp.exp(old - mx), jnp.exp(lse - mx)
            mst[h, 0, :, 0:rows] = mx
            lst[h, 0, :, 0:rows] = lst[h, 0, :, 0:rows] * fade + gain
            ast[h, 0, :, 0:rows] = ast[h, 0, :, 0:rows] * fade[0:1] + pbuf[j, h].astype(F32) * gain[0:1]

        done = ast[h, 0, :, 0:rows] * (1.0 / lst[h, 0, 0:1, 0:rows])
        return done.T.astype(BF)

    @pl.loop(0, heads // 2)
    def _(c):
        att[c, :, 0:HD] = one_head(2 * c)
        att[c, :, HD:2 * HD] = one_head(2 * c + 1)

        @pl.when(c == 0)
        def _():
            local_w.wait()

        @pl.when(c < heads // 2 - 1)
        def _():
            lhs = att[c]

            @pl.loop(0, m)
            def _(b):
                at = pl.ds(pl.multiple_of(b * cols, cols), cols)
                acc[b] += dot(lhs, wv[pl.ds(pl.multiple_of(c * 2 * HD, 2 * HD), 2 * HD), at])

    pieces = 4
    piece = cols // pieces

    def across(d, i):
        return remote(s1.at[d, i], r1.at[d, i], a_s.at[d, i], a_r.at[d, i], "mp", partner)

    def along(d, i):
        there = lax.rem(chip + d, chips) * 2 + core
        return remote(s2.at[d, i], r2.at[d, i], b_s.at[d, i], b_r.at[d, i], "mp", there)

    last = att[heads // 2 - 1]

    def summed(b, i):
        at = pl.ds(pl.multiple_of(b * cols + i * piece, piece), piece)
        return acc[b, :, i * piece:(i + 1) * piece] + dot(last, wv[channels - 2 * HD:, at])

    def block(d, side):
        return lax.rem(chip + d, chips) * 2 + side

    order = [d % chips for d in range(1, chips + 1)]
    for d in order:
        for i in range(pieces):
            s1[d, i] = summed(block(d, 1 - core), i).astype(BF)
            across(d, i).start()
    for d in range(1, chips):
        for i in range(pieces):
            total = summed(block(d, core), i)
            across(d, i).wait_recv()
            s2[d, i] = (total + r1[d, i].astype(F32)).astype(BF)
            along(d, i).start()
    for i in range(pieces):
        acc[me, :, i * piece:(i + 1) * piece] = summed(me, i)
    for i in range(pieces):
        across(0, i).wait_recv()
        acc[me, :, i * piece:(i + 1) * piece] += r1[0, i].astype(F32)
    for i in range(pieces):
        total = acc[me, :, i * piece:(i + 1) * piece]
        for d in range(1, chips):
            along(d, i).wait_recv()
            total = total + r2[d, i].astype(F32)
        out_ref[:, i * piece:(i + 1) * piece] = total.astype(BF)

    for i in range(pieces):
        for d in range(chips):
            across(d, i).wait_send()
        for d in range(1, chips):
            along(d, i).wait_send()

    @pl.when(z < n - 1)
    def _():
        rim.wait_send()

    @pl.loop(0, heads)
    def _(h):
        def ended(s, o, t):
            o.wait_send()
            t.wait_send()
        @pl.when(z < n - 1)
        def _():
            gate(h).wait_send()

        each_query(h, lambda c: c.wait_send())
        each_key(h, lambda c: c.wait_send())
        each_value(h, lambda c: c.wait_send())
        each_part(h, ended)


def per_device(n, m, inputs, short_filter, long_filter, skip_gain, queries, key_rows, out_weight):
    rows, _, channels = inputs.shape
    heads = channels // HD
    groups = long_filter.shape[0]
    total = out_weight.shape[1]
    cols = total // m
    chips = m // 2
    pivot = n // 3
    slots = n - pivot
    batch = min(3, slots)
    padded = -(-slots // batch) * batch
    span = batch * rows
    gq = padded // batch
    parts = max(slots - 1, 1)
    vm = pltpu.VMEM
    dma = pltpu.SemaphoreType.DMA
    scratch = [
        vm(short_filter.shape, BF), vm(long_filter.shape, BF), vm((1, channels), F32), dma((3,)),
        vm((3, rows, channels), BF), vm((16, channels), BF), vm((16, channels), BF),
        vm((heads, rows, HD), F32), vm((heads, rows, HD), BF), vm((heads, rows, HD), BF),
        vm((groups, rows, 2 * rows), BF),
        vm((pivot + 1, heads, rows, HD), BF), vm((pivot + 1, heads, HD, rows), BF),
        vm((heads, padded * rows, HD), BF),
        vm((heads, gq, 8, span), F32), vm((heads, gq, 8, span), F32), vm((heads, gq, HD, span), F32),
        vm((parts, heads, HD, rows), BF), vm((parts, heads, 1, rows), F32),
        vm((parts, heads, HD, rows), BF), vm((parts, heads, 1, rows), F32),
        vm((heads // 2, rows, 2 * HD), BF), vm((channels, total), BF), vm((m, rows, cols), F32),
    ] + [vm((chips, 4, rows, cols // 4), BF)] * 4 + [
        dma, dma((heads,)), dma((heads,)), dma, dma, dma, dma((heads,)), dma((heads,)),
    ] + [dma((pivot + 1, heads))] * 4 + [dma((slots, heads))] * 2 + [
        dma((parts, heads)), dma((parts, heads)), dma((parts, heads)), dma((parts, heads)),
    ] + [dma((chips, 4))] * 4
    in_vmem = pl.BlockSpec(memory_space=pltpu.VMEM)
    in_hbm = pl.BlockSpec(memory_space=pl.ANY)
    return pl.pallas_call(
        functools.partial(kernel, n, m),
        out_shape=pltpu.VMEM((rows, cols), BF),
        in_specs=[in_hbm] * 7,
        out_specs=in_vmem,
        scratch_shapes=scratch,
        compiler_params=pltpu.CompilerParams(
            collective_id=0, has_side_effects=True, vmem_limit_bytes=60 * 2**20),
    )(inputs.transpose(1, 0, 2), short_filter, long_filter, skip_gain[None], queries, key_rows, out_weight)


def solution(mesh):
    placed = (
        P(("parts", "ctx"), None, "mp"),
        P(None, None, "mp"),
        P("mp", None),
        P("mp"),
        P(("parts", "ctx"), "mp"),
        P(("parts", "ctx"), "mp"),
        P("mp", None),
    )
    return jax.shard_map(
        functools.partial(per_device, mesh.shape["ctx"], mesh.shape["mp"]),
        mesh=mesh, in_specs=placed, out_specs=P(("parts", "ctx"), "mp"), check_vma=False)
```
